256 devices in a mesh: kocc: 16 (over y_lo, z), vrow: 16 (over y_hi, x, core).
Axes of the slice: x: 4, y: 4 (y_hi: 2, y_lo: 2; y = y_hi * 2 + y_lo), z: 8, core: 2. Of those that a mesh axis runs over, the one named last changes fastest.
Arguments:
- factors: bfloat16 [16, 16, 128, 1536], P('kocc', None, 'vrow'), may hold values from -0.125 to 0.125
- amps: bfloat16 [4, 16, 16, 128, 4096], P(None, 'kocc', None, None, 'vrow'), may hold values from -6 to 6
- eps_occ: float32 [16, 16], P('kocc'), may hold values from -1 to -0.3
- eps_vir: bfloat16 [16, 128], P('kocc'), may hold values from 0.099609375 to 1
- col_energy: float32 [4096], P('vrow'), may hold values from 0.2 to 1.5
- q_index: int32 [1], replicated, may hold values from 1 to 15
Outputs:
- sigma: bfloat16 [4, 16, 16, 128, 4096], P(None, 'kocc', None, None, 'vrow')
The draws below stay inside these ranges and needn't reach their ends.
All inputs are finite; a program needn't handle non-finite values.
Results may differ from the reference program's by a relative error of at most 0.015.
Values may be sent and summed in bfloat16 or wider, within the bound.
No kernel may reach another device: no remote copies, remote signals or barrier semaphores. Data moves between devices by JAX's collectives and lax.ppermute only.
A program may use at most 128 MiB of HBM per device.

```python
import jax
import jax.numpy as jnp
from jax import lax

NO = 16
NV = 128
NAUX = 1536
ROOTS = 4
NK = 16
J = 4096


def block_scale(key, shape, shards, least, largest):
    def one(position, blocks):
        draws = jax.random.uniform(jax.random.fold_in(jax.random.fold_in(key, 6), position), (blocks,), jnp.float32, least / len(shards), largest / len(shards))
        return jnp.repeat(jnp.exp(draws), shape[position] // blocks).reshape((-1,) + (1,) * (len(shape) - position - 1))

    loudness = one(*shards[0])
    for cut in shards[1:]:
        loudness = loudness * one(*cut)
    return loudness


def centred(key, extent, deviation, bound, cuts=(), kind=jnp.bfloat16):
    entries = jax.random.normal(key, extent, jnp.float32) * deviation
    if len(cuts) > 0:
        entries = block_scale(key, extent, cuts, -0.22, 0.18) * entries
    return jnp.clip(entries, min=-bound, max=bound).astype(kind)


def setup_inputs(seed: int = 0) -> dict:
    key_of = jax.random.split(jax.random.key(seed), 7)
    factors = centred(key_of[0], (NK, NO, NV, NAUX), (NV * NK) ** -0.5, 0.125, ((0, 16), (2, 16)))
    amps = centred(key_of[1], (ROOTS, NK, NO, NV, J), 1.0, 6.0, ((1, 16), (4, 16)))
    eps_occ = jnp.clip(-1.0 + 0.7 * jax.random.uniform(key_of[2], (NK, NO), jnp.float32) ** block_scale(key_of[2], (NK, NO), ((0, 16),), -0.2, 0.2), -1.0, -0.3)
    eps_vir = jnp.clip(0.099609375 + 0.9003906 * jax.random.uniform(key_of[3], (NK, NV), jnp.float32) ** block_scale(key_of[3], (NK, NV), ((0, 16),), -0.2, 0.2), 0.099609375, 1.0).astype(jnp.bfloat16)
    col_energy = jnp.clip(0.2 + 1.3 * jax.random.uniform(key_of[4], (J,), jnp.float32) ** block_scale(key_of[4], (J,), ((0, 16),), -0.2, 0.2), 0.2, 1.5)
    q_index = jax.random.randint(key_of[5], (1,), 1, NK).astype(jnp.int32)
    return dict(factors=factors, amps=amps, eps_occ=eps_occ, eps_vir=eps_vir, col_energy=col_energy, q_index=q_index)


def reference(factors, amps, eps_occ, eps_vir, col_energy, q_index):
    momenta = jnp.arange(NK, dtype=jnp.int32)
    source = jnp.mod(momenta - q_index[0], NK).astype(jnp.int32)
    shifted = factors[source]
    vir_shift = eps_vir[source]
    factor_rows = shifted.reshape(NK * NO * NV, NAUX)
    amp_rows = amps.reshape(ROOTS, NK * NO * NV, J)
    cycle = lax.map(lambda amp_block: jnp.dot(factor_rows.T, amp_block, preferred_element_type=jnp.float32), amp_rows)
    cycle_b = cycle.astype(jnp.bfloat16)

    def per_point(inputs):
        point_factor, point_vir, point_occ, point_amps = inputs
        cycle_part = jnp.einsum('np,rpj->rnj', point_factor.reshape(NO * NV, NAUX).astype(jnp.float32), cycle_b.astype(jnp.float32))
        cycle_part = cycle_part.reshape(ROOTS, NO, NV, J)
        energy_gap = point_vir.astype(jnp.float32)[None, :, None] - point_occ[:, None, None] + col_energy[None, None, :]
        return (cycle_part + energy_gap[None] * point_amps.astype(jnp.float32)).astype(jnp.bfloat16)

    result = lax.map(per_point, (shifted, vir_shift, eps_occ, jnp.moveaxis(amps, 1, 0)))
    return jnp.moveaxis(result, 0, 1)
```

```python
import functools

import jax
import jax.numpy as jnp
from jax import lax
from jax.experimental import pallas as pl
from jax.experimental.pallas import tpu as pltpu
from jax.sharding import Mesh
from jax.sharding import PartitionSpec as P

CHUNKS = 4


def route(sizes, step):
    pairs = []
    total = 1
    for size in sizes:
        total *= size
    for flat in range(total):
        rest, coords = flat, []
        for size in reversed(sizes):
            coords.insert(0, rest % size)
            rest //= size
        target = 0
        for size, coord in zip(sizes, step(*coords)):
            target = target * size + coord % size
        pairs.append((flat, target))
    return pairs


def swap(block, axis):
    return lax.ppermute(block, axis, [(0, 1), (1, 0)])


def ring(block, axis):
    sizes = (lax.axis_size(axis), lax.axis_size("core"))
    return lax.ppermute(block, (axis, "core"), route(sizes, lambda i, c: (i + 1 - 2 * c, c)))


def shift(factors, eps_vir, q):
    sizes = lax.axis_size("y_lo") * lax.axis_size("z")

    def by(distance):
        def branch(block, row):
            if distance == 0:
                return block, row
            pairs = [(i, (i + distance) % sizes) for i in range(sizes)]
            return lax.ppermute((block, row), ("y_lo", "z"), pairs)

        return branch

    return lax.switch(jnp.mod(q, sizes), [by(d) for d in range(sizes)], factors, eps_vir)


def merge(core, mine, other):
    mine, other = mine.astype(jnp.float32), other.astype(jnp.float32)
    first = jnp.where(core == 0, mine, other)
    second = jnp.where(core == 0, other, mine)
    both = jnp.concatenate([first, second], axis=1)
    return both.reshape(both.shape[0] * both.shape[1], both.shape[2]).astype(jnp.bfloat16)


def dot1_kernel(table, mine, other, amps, out, total):
    step = pl.program_id(0)
    rows = merge(table[0], mine[0], other[0])
    roots = amps.shape[0]

    @pl.when(step == 0)
    def _():
        total[...] = jnp.zeros_like(total)

    for root in range(roots):
        block = amps[root].reshape(rows.shape[0], amps.shape[-1])
        total[root] += lax.dot_general(rows, block, (((0,), (0,)), ((), ())), preferred_element_type=jnp.float32)

    @pl.when(step == pl.num_programs(0) - 1)
    def _():
        out[...] = total[...].astype(out.dtype)


def dot2_kernel(chunks, table, *refs):
    mine, other, cycle = refs[:chunks], refs[chunks : 2 * chunks], refs[2 * chunks : 3 * chunks]
    amps, occ, vir, col, out = refs[3 * chunks :]
    roots, points, block, columns = amps.shape
    pieces = cycle[0].shape[0]
    each = pieces // roots
    total = [None] * roots
    for c in range(chunks):
        rows = merge(table[0], mine[c][0], other[c][0])
        for root in range(roots):
            parts = [cycle[c][table[1 + root * each + e]] for e in range(each)]
            term = jnp.dot(rows, jnp.concatenate(parts, axis=0), preferred_element_type=jnp.float32)
            total[root] = term if c == 0 else total[root] + term
    gap = vir[0][None] - occ[...] + col[...][None]
    for root in range(roots):
        cyc = total[root].reshape(points, block, columns)
        out[root] = (cyc + gap * amps[root].astype(jnp.float32)).astype(out.dtype)


def shards(factors, amps, eps_occ, eps_vir, col_energy, q_index):
    y_hi, x, core, z = (lax.axis_index(a) for a in ("y_hi", "x", "core", "z"))
    x_count, z_count, y_count = lax.axis_size("x"), lax.axis_size("z"), lax.axis_size("y_hi")
    amp_local = amps[:, 0]
    roots, points, virtuals, columns = amp_local.shape
    aux = factors.shape[3]
    width = aux // CHUNKS
    up = 1 - 2 * core

    shifted, vir_row = shift(factors[0], eps_vir, q_index[0])
    share = shifted.shape[1]
    pair = 2 * share
    blocks = virtuals // pair

    arrival = [(h, s) for h in range(y_count) for s in range(x_count)]
    places = jnp.stack([jnp.mod(y_hi + h, y_count) * x_count + jnp.mod(x - up * s, x_count) for h, s in arrival])
    order = jnp.mod((z - jnp.arange(z_count)) * up, z_count)
    table = jnp.concatenate([core[None], order, places]).astype(jnp.int32)
    base = 1 + z_count

    def twin(p):
        h, s = p // x_count, p % x_count
        return h * x_count + lax.rem(x_count - s, x_count)

    mine_spec = pl.BlockSpec((1, points, share, width), lambda p, t: (p, 0, 0, 0))
    other_spec = pl.BlockSpec((1, points, share, width), lambda p, t: (twin(p), 0, 0, 0))
    amp_spec = pl.BlockSpec((roots, points, pair, columns), lambda p, t: (0, 0, t[base + p], 0))

    dot1 = pl.pallas_call(
        dot1_kernel,
        out_shape=jax.ShapeDtypeStruct((roots, width, columns), jnp.bfloat16),
        grid_spec=pltpu.PrefetchScalarGridSpec(
            num_scalar_prefetch=1,
            grid=(blocks,),
            in_specs=[mine_spec, other_spec, amp_spec],
            out_specs=pl.BlockSpec((roots, width, columns), lambda p, t: (0, 0, 0)),
            scratch_shapes=[pltpu.VMEM((roots, width, columns), jnp.float32)],
        ),
        compiler_params=pltpu.CompilerParams(vmem_limit_bytes=32 << 20),
        cost_estimate=pl.CostEstimate(
            flops=2 * points * virtuals * width * roots * columns,
            bytes_accessed=2 * points * virtuals * (width + roots * columns),
            transcendentals=0,
        ),
        name="dot1",
    )

    gathered, cycles = [], []
    for c in range(CHUNKS):
        own = shifted[:, :, c * width : (c + 1) * width]
        far = swap(own, "y_hi")
        pieces = []
        for block in (own, far):
            pieces.append(block)
            for _ in range(x_count - 1):
                block = ring(block, "x")
                pieces.append(block)
        mine = jnp.stack(pieces)
        other = swap(mine, "core")
        gathered.append((mine, other))
        terms = dot1(table, mine, other, amp_local).reshape(z_count, -1, columns)

        def piece(i):
            return lax.dynamic_index_in_dim(terms, jnp.mod(i, z_count), 0, keepdims=False)

        total = piece(z - up)
        for s in range(1, z_count):
            total = ring(total, "z").astype(jnp.float32) + piece(z - up * (s + 1)).astype(jnp.float32)
            total = total.astype(jnp.bfloat16)
        total = (total.astype(jnp.float32) + swap(total, "y_lo").astype(jnp.float32)).astype(jnp.bfloat16)
        parts = [total]
        for _ in range(z_count - 1):
            parts.append(ring(parts[-1], "z"))
        cycles.append(jnp.stack(parts))

    occ = eps_occ[0].reshape(points, 1, 1)
    vir = vir_row[0].astype(jnp.float32).reshape(blocks, pair, 1)
    col = col_energy.reshape(1, columns)
    whole = lambda shape: pl.BlockSpec(shape, lambda p, t: (0,) * len(shape))
    sigma = pl.pallas_call(
        functools.partial(dot2_kernel, CHUNKS),
        out_shape=jax.ShapeDtypeStruct(amp_local.shape, jnp.bfloat16),
        grid_spec=pltpu.PrefetchScalarGridSpec(
            num_scalar_prefetch=1,
            grid=(blocks,),
            in_specs=[mine_spec] * CHUNKS
            + [other_spec] * CHUNKS
            + [whole(cycles[0].shape)] * CHUNKS
            + [amp_spec, whole(occ.shape), pl.BlockSpec((1, pair, 1), lambda p, t: (t[base + p], 0, 0)), whole(col.shape)],
            out_specs=amp_spec,
        ),
        compiler_params=pltpu.CompilerParams(vmem_limit_bytes=48 << 20),
        cost_estimate=pl.CostEstimate(
            flops=2 * points * virtuals * aux * roots * columns,
            bytes_accessed=2 * (points * virtuals * (aux + 2 * roots * columns) + aux * roots * columns),
            transcendentals=0,
        ),
        name="dot2",
    )(table, *[m for m, _ in gathered], *[o for _, o in gathered], *cycles, amp_local, occ, vir, col)
    return sigma[:, None]


def solution(mesh):
    split = Mesh(mesh.devices.reshape(2, 8, 2, 4, 2), ("y_lo", "z", "y_hi", "x", "core"))
    kocc, vrow = ("y_lo", "z"), ("y_hi", "x", "core")
    in_specs = (
        P(kocc, None, vrow, None),
        P(None, kocc, None, None, vrow),
        P(kocc, None),
        P(kocc, None),
        P(vrow),
        P(),
    )
    out_specs = P(None, kocc, None, None, vrow)
    return jax.shard_map(shards, mesh=split, in_specs=in_specs, out_specs=out_specs, check_vma=False)
```

```python
import functools

import jax
import jax.numpy as jnp
from jax import lax
from jax.experimental import pallas as pl
from jax.experimental.pallas import tpu as pltpu
from jax.sharding import Mesh
from jax.sharding import PartitionSpec as P

CHUNKS = 2


def route(sizes, step):
    pairs = []
    total = 1
    for size in sizes:
        total *= size
    for flat in range(total):
        rest, coords = flat, []
        for size in reversed(sizes):
            coords.insert(0, rest % size)
            rest //= size
        target = 0
        for size, coord in zip(sizes, step(*coords)):
            target = target * size + coord % size
        pairs.append((flat, target))
    return pairs


def swap(block, axis):
    return lax.ppermute(block, axis, [(0, 1), (1, 0)])


def ring(block, axis, way=1):
    sizes = (lax.axis_size(axis), lax.axis_size("core"))
    return lax.ppermute(block, (axis, "core"), route(sizes, lambda i, c: (i + way * (1 - 2 * c), c)))


def ring_gather(block, axis):
    size = lax.axis_size(axis)
    ahead, behind = [block], [block]
    for _ in range(size // 2):
        ahead.append(ring(ahead[-1], axis))
    for _ in range((size - 1) // 2):
        behind.append(ring(behind[-1], axis, -1))
    return ahead + behind[:0:-1]


def add(*terms):
    return sum(t.astype(jnp.float32) for t in terms).astype(jnp.bfloat16)


def ring_reduce(piece, place, up, axis):
    size = lax.axis_size(axis)
    sums = []
    for way, steps in ((1, size // 2), (-1, (size - 1) // 2)):
        total = piece(place + way * up * steps)
        for s in range(1, steps + 1):
            total = ring(total, axis, way)
            if s < steps:
                total = add(total, piece(place + way * up * (steps - s)))
        sums.append(total)
    return add(piece(place), *sums)


def shift(block, q):
    sizes = lax.axis_size("y_lo") * lax.axis_size("z")

    def by(distance):
        pairs = [(i, (i + distance) % sizes) for i in range(sizes)]
        return lambda b: lax.ppermute(b, ("y_lo", "z"), pairs) if distance else b

    return lax.switch(jnp.mod(q, sizes), [by(d) for d in range(sizes)], block)


def turn_kernel(table, amps, out):
    roots, points, share, columns = amps.shape
    for root in range(roots):
        rows = amps[root].astype(jnp.float32).reshape(points * share, columns)
        out[root * columns : (root + 1) * columns] = rows.T.astype(out.dtype)


def dot2_kernel(chunks, pieces, table, *refs):
    halves = (refs[:chunks], refs[chunks : 2 * chunks])
    parts = refs[2 * chunks : 2 * chunks + chunks * pieces]
    amps, occ, vir, col, out, cycle = refs[2 * chunks + chunks * pieces :]
    _, points, _, columns = amps.shape
    share = vir.shape[1]
    each = columns // parts[0].shape[0]
    root = pl.program_id(0)

    @pl.when(root == 0)
    def _():
        for c in range(chunks):
            for s in range(pieces):
                cycle[c, table[s]] = parts[c * pieces + s][...]

    for h, half in enumerate(halves):
        total = 0.0
        for c in range(chunks):
            weights = cycle[c, pl.ds(root * each, each)].reshape(columns, cycle.shape[3])
            total += lax.dot_general(half[c][...], weights, (((1,), (1,)), ((), ())), preferred_element_type=jnp.float32)
        count = total.shape[0] // (points * share)
        for p in range(count):
            place = table[pieces + h * count + p]
            rows = pl.ds(pl.multiple_of(place * share, share), share)
            gap = vir[place][None] - occ[...] + col[...][None]
            cyc = total[p * points * share : (p + 1) * points * share].reshape(points, share, columns)
            out[0, :, rows, :] = (cyc + gap * amps[0, :, rows, :].astype(jnp.float32)).astype(out.dtype)


def shards(factors, amps, eps_occ, eps_vir, col_energy, q_index):
    y_hi, x, core, z = (lax.axis_index(a) for a in ("y_hi", "x", "core", "z"))
    x_count, z_count, y_count = lax.axis_size("x"), lax.axis_size("z"), lax.axis_size("y_hi")
    amp_local = amps[:, 0]
    roots, points, virtuals, columns = amp_local.shape
    aux = factors.shape[3]
    width = aux // CHUNKS
    up = 1 - 2 * core

    share = factors.shape[2]
    places_count = virtuals // share
    held = points * share
    row = jnp.broadcast_to(jnp.pad(eps_vir, ((0, 0), (0, aux - virtuals))), (share, aux))
    shifted = shift(jnp.concatenate([factors[0].reshape(held, aux), row]), q_index[0])
    vir = shifted[held, :virtuals].astype(jnp.float32).reshape(places_count, share, 1)

    places = []
    for sign, own_core in ((up, core), (-up, 1 - core)):
        for h in range(y_count):
            for s in range(x_count):
                chip = jnp.mod(y_hi + h, y_count) * x_count + jnp.mod(x - sign * s, x_count)
                places.append(chip * 2 + own_core)
    order = [jnp.mod(z - up * s, z_count) for s in range(z_count)]
    table = jnp.stack(order + places).astype(jnp.int32)

    turned = pl.pallas_call(
        turn_kernel,
        out_shape=jax.ShapeDtypeStruct((roots * columns, points * virtuals), jnp.bfloat16),
        grid_spec=pltpu.PrefetchScalarGridSpec(
            num_scalar_prefetch=1,
            grid=(places_count,),
            in_specs=[pl.BlockSpec((roots, points, share, columns), lambda p, t: (0, 0, t[z_count + p], 0))],
            out_specs=pl.BlockSpec((roots * columns, held), lambda p, t: (0, p)),
        ),
        cost_estimate=pl.CostEstimate(flops=0, bytes_accessed=4 * roots * columns * points * virtuals, transcendentals=0),
        name="turn",
    )(table, amp_local)
    half = places_count // 2 * held

    mines, others, parts = [], [], []
    for c in range(CHUNKS):
        own = shifted[:held, c * width : (c + 1) * width]
        far = swap(own, "y_hi")
        mine = jnp.concatenate(ring_gather(own, "x") + ring_gather(far, "x"))
        other = swap(mine, "core")
        mines.append(mine)
        others.append(other)
        terms = jnp.dot(turned[:, :half], mine, preferred_element_type=jnp.float32)
        terms += jnp.dot(turned[:, half:], other, preferred_element_type=jnp.float32)
        terms = terms.astype(jnp.bfloat16).reshape(z_count, -1, width)

        def piece(i):
            return lax.dynamic_index_in_dim(terms, jnp.mod(i, z_count), 0, keepdims=False)

        total = ring_reduce(piece, z, up, "z")
        total = add(total, swap(total, "y_lo"))
        parts += ring_gather(total, "z")

    occ = eps_occ[0].reshape(points, 1, 1)
    col = col_energy.reshape(1, columns)
    whole = lambda a: pl.BlockSpec(a.shape, lambda r, t: (0,) * a.ndim)
    root_spec = pl.BlockSpec((1, points, virtuals, columns), lambda r, t: (r, 0, 0, 0))
    held_arrays = [*mines, *others, *parts]
    sigma = pl.pallas_call(
        functools.partial(dot2_kernel, CHUNKS, z_count),
        out_shape=jax.ShapeDtypeStruct(amp_local.shape, jnp.bfloat16),
        grid_spec=pltpu.PrefetchScalarGridSpec(
            num_scalar_prefetch=1,
            grid=(roots,),
            in_specs=[pl.BlockSpec(memory_space=pltpu.VMEM)] * len(held_arrays) + [root_spec, whole(occ), whole(vir), whole(col)],
            out_specs=root_spec,
            scratch_shapes=[pltpu.VMEM((CHUNKS, z_count, *parts[0].shape), jnp.bfloat16)],
        ),
        compiler_params=pltpu.CompilerParams(vmem_limit_bytes=48 << 20),
        cost_estimate=pl.CostEstimate(
            flops=2 * points * virtuals * aux * roots * columns,
            bytes_accessed=2 * (points * virtuals * (aux + 2 * roots * columns) + aux * roots * columns),
            transcendentals=0,
        ),
        name="dot2",
    )(table, *held_arrays, amp_local, occ, vir, col)
    return sigma[:, None]


def solution(mesh):
    split = Mesh(mesh.devices.reshape(2, 8, 2, 4, 2), ("y_lo", "z", "y_hi", "x", "core"))
    kocc, vrow = ("y_lo", "z"), ("y_hi", "x", "core")
    in_specs = (
        P(kocc, None, vrow, None),
        P(None, kocc, None, None, vrow),
        P(kocc, None),
        P(kocc, None),
        P(vrow),
        P(),
    )
    out_specs = P(None, kocc, None, None, vrow)
    return jax.shard_map(shards, mesh=split, in_specs=in_specs, out_specs=out_specs, check_vma=False)
```

```python
import functools

import jax
import jax.numpy as jnp
from jax import lax
from jax.experimental import pallas as pl
from jax.experimental.pallas import tpu as pltpu
from jax.sharding import Mesh
from jax.sharding import PartitionSpec as P

CHUNKS = 2


def route(sizes, step):
    pairs = []
    total = 1
    for size in sizes:
        total *= size
    for flat in range(total):
        rest, coords = flat, []
        for size in reversed(sizes):
            coords.insert(0, rest % size)
            rest //= size
        target = 0
        for size, coord in zip(sizes, step(*coords)):
            target = target * size + coord % size
        pairs.append((flat, target))
    return pairs


def swap(block, axis):
    return lax.ppermute(block, axis, [(0, 1), (1, 0)])


def ring(block, axis, way=1):
    sizes = (lax.axis_size(axis), lax.axis_size("core"))
    return lax.ppermute(block, (axis, "core"), route(sizes, lambda i, c: (i + way * (1 - 2 * c), c)))


def ring_gather(block, axis):
    size = lax.axis_size(axis)
    ahead, behind = [block], [block]
    for _ in range(size // 2):
        ahead.append(ring(ahead[-1], axis))
    for _ in range((size - 1) // 2):
        behind.append(ring(behind[-1], axis, -1))
    return ahead + behind[:0:-1]


def add(*terms):
    return sum(t.astype(jnp.float32) for t in terms).astype(jnp.bfloat16)


def ring_reduce(piece, place, up, axis):
    size = lax.axis_size(axis)
    sums = []
    for way, steps in ((1, size // 2), (-1, (size - 1) // 2)):
        total = piece(place + way * up * steps)
        for s in range(1, steps + 1):
            total = ring(total, axis, way)
            if s < steps:
                total = add(total, piece(place + way * up * (steps - s)))
        sums.append(total)
    return add(piece(place), *sums)


def shift(block, q):
    sizes = lax.axis_size("y_lo") * lax.axis_size("z")

    def by(distance):
        pairs = [(i, (i + distance) % sizes) for i in range(sizes)]
        return lambda b: lax.ppermute(b, ("y_lo", "z"), pairs) if distance else b

    return lax.switch(jnp.mod(q, sizes), [by(d) for d in range(sizes)], block)


def turn_kernel(table, near, far, near_out, far_out):
    for amps, out in ((near, near_out), (far, far_out)):
        roots, points, share, columns = amps.shape
        for root in range(roots):
            rows = amps[root].astype(jnp.float32).reshape(points * share, columns)
            out[root * columns : (root + 1) * columns] = rows.T.astype(out.dtype)


def dot2_kernel(pieces, table, mine, other, *refs):
    parts, (amps, occ, vir, col) = refs[:pieces], refs[pieces : pieces + 4]
    out, cycle = refs[-2:]
    _, points, _, columns = amps.shape
    share = vir.shape[1]
    each = columns // parts[0].shape[0]
    step = pl.program_id(0)

    @pl.when(step == 0)
    def _():
        for s in range(pieces):
            cycle[table[s]] = parts[s][...]

    weights = cycle[pl.ds(step * each, each)].reshape(columns, cycle.shape[2])
    for h, half in enumerate((mine, other)):
        total = lax.dot_general(half[...], weights, (((1,), (1,)), ((), ())), preferred_element_type=jnp.float32)
        count = total.shape[0] // (points * share)
        for p in range(count):
            place = table[pieces + h * count + p]
            rows = pl.ds(pl.multiple_of(place * share, share), share)
            gap = vir[place][None] - occ[...] + col[...][None]
            cyc = total[p * points * share : (p + 1) * points * share].reshape(points, share, columns)
            out[0, :, rows, :] = (cyc + gap * amps[0, :, rows, :].astype(jnp.float32)).astype(out.dtype)


def shards(factors, amps, eps_occ, eps_vir, col_energy, q_index):
    y_hi, x, core, z = (lax.axis_index(a) for a in ("y_hi", "x", "core", "z"))
    x_count, z_count, y_count = lax.axis_size("x"), lax.axis_size("z"), lax.axis_size("y_hi")
    amp_local = amps[:, 0]
    roots, points, virtuals, columns = amp_local.shape
    aux = factors.shape[3]
    up = 1 - 2 * core

    share = factors.shape[2]
    places_count = virtuals // share
    held = points * share
    row = jnp.broadcast_to(jnp.pad(eps_vir, ((0, 0), (0, aux - virtuals))), (share, aux))
    shifted = shift(jnp.concatenate([factors[0].reshape(held, aux), row]), q_index[0])
    vir = shifted[held, :virtuals].astype(jnp.float32).reshape(places_count, share, 1)

    places = []
    for sign, own_core in ((up, core), (-up, 1 - core)):
        for h in range(y_count):
            for s in range(x_count):
                chip = jnp.mod(y_hi + h, y_count) * x_count + jnp.mod(x - sign * s, x_count)
                places.append(chip * 2 + own_core)
    order = [jnp.mod(z - up * s, z_count) for s in range(z_count)]
    table = jnp.stack(order + places).astype(jnp.int32)

    half = places_count // 2
    turn_spec = lambda first: pl.BlockSpec((roots, points, share, columns), lambda p, t: (0, 0, t[z_count + first + p], 0))
    turn = pl.pallas_call(
        turn_kernel,
        out_shape=[jax.ShapeDtypeStruct((roots * columns, half * held), jnp.bfloat16)] * 2,
        grid_spec=pltpu.PrefetchScalarGridSpec(
            num_scalar_prefetch=1,
            grid=(half,),
            in_specs=[turn_spec(0), turn_spec(half)],
            out_specs=[pl.BlockSpec((roots * columns, held), lambda p, t: (0, p))] * 2,
        ),
        compiler_params=pltpu.CompilerParams(vmem_limit_bytes=16 << 20),
        cost_estimate=pl.CostEstimate(flops=0, bytes_accessed=4 * roots * columns * points * virtuals, transcendentals=0),
        name="turn",
    )

    own = shifted[:held]
    far = swap(own, "y_hi")
    ahead, behind = ring(own, "x"), ring(own, "x", -1)
    amp_turned, _ = lax.optimization_barrier((amp_local, own))
    near_amps, far_amps = turn(table, amp_turned, amp_turned)
    near_amps, far_amps, ahead, far = lax.optimization_barrier((near_amps, far_amps, ahead, far))
    mine = jnp.concatenate([own, ahead, ring(ahead, "x"), behind] + ring_gather(far, "x"))
    other = swap(mine, "core")
    near_terms = jnp.dot(near_amps, mine, preferred_element_type=jnp.float32)

    occ = eps_occ[0].reshape(points, 1, 1)
    col = col_energy.reshape(1, columns)
    whole = lambda a: pl.BlockSpec(a.shape, lambda r, t: (0,) * a.ndim)
    in_vmem = pl.BlockSpec(memory_space=pltpu.VMEM)
    group = roots // CHUNKS

    sigma = None
    for c in range(CHUNKS):
        lines = slice(c * group * columns, (c + 1) * group * columns)
        terms = near_terms[lines] + jnp.dot(far_amps[lines], other, preferred_element_type=jnp.float32)
        terms = terms.astype(jnp.bfloat16).reshape(z_count, -1, aux)

        def piece(i):
            return lax.dynamic_index_in_dim(terms, jnp.mod(i, z_count), 0, keepdims=False)

        total = ring_reduce(piece, z, up, "z")
        total = add(total, swap(total, "y_lo"))
        parts = ring_gather(total, "z")

        root_spec = pl.BlockSpec((1, points, virtuals, columns), lambda r, t, first=c * group: (r + first, 0, 0, 0))
        before = [] if sigma is None else [sigma]
        sigma = pl.pallas_call(
            functools.partial(dot2_kernel, z_count),
            out_shape=jax.ShapeDtypeStruct(amp_local.shape, jnp.bfloat16),
            grid_spec=pltpu.PrefetchScalarGridSpec(
                num_scalar_prefetch=1,
                grid=(group,),
                in_specs=[in_vmem] * (2 + z_count)
                + [root_spec, whole(occ), whole(vir), whole(col)]
                + [pl.BlockSpec(memory_space=pl.ANY)] * len(before),
                out_specs=root_spec,
                scratch_shapes=[pltpu.VMEM((z_count, *parts[0].shape), jnp.bfloat16)],
            ),
            input_output_aliases={} if sigma is None else {7 + z_count: 0},
            compiler_params=pltpu.CompilerParams(vmem_limit_bytes=16 << 20),
            cost_estimate=pl.CostEstimate(
                flops=2 * points * virtuals * aux * group * columns,
                bytes_accessed=2 * (points * virtuals * (aux + 2 * group * columns) + aux * group * columns),
                transcendentals=0,
            ),
            name="dot2",
        )(table, mine, other, *parts, amp_local, occ, vir, col, *before)
    return sigma[:, None]


def solution(mesh):
    split = Mesh(mesh.devices.reshape(2, 8, 2, 4, 2), ("y_lo", "z", "y_hi", "x", "core"))
    kocc, vrow = ("y_lo", "z"), ("y_hi", "x", "core")
    in_specs = (
        P(kocc, None, vrow, None),
        P(None, kocc, None, None, vrow),
        P(kocc, None),
        P(kocc, None),
        P(vrow),
        P(),
    )
    out_specs = P(None, kocc, None, None, vrow)
    return jax.shard_map(shards, mesh=split, in_specs=in_specs, out_specs=out_specs, check_vma=False)
```

```python
import functools

import jax
import jax.numpy as jnp
from jax import lax
from jax.experimental import pallas as pl
from jax.experimental.pallas import tpu as pltpu
from jax.sharding import Mesh
from jax.sharding import PartitionSpec as P

CHUNKS = 2


def route(sizes, step):
    pairs = []
    total = 1
    for size in sizes:
        total *= size
    for flat in range(total):
        rest, coords = flat, []
        for size in reversed(sizes):
            coords.insert(0, rest % size)
            rest //= size
        target = 0
        for size, coord in zip(sizes, step(*coords)):
            target = target * size + coord % size
        pairs.append((flat, target))
    return pairs


def swap(block, axis):
    return lax.ppermute(block, axis, [(0, 1), (1, 0)])


def ring(block, axis, way=1):
    sizes = (lax.axis_size(axis), lax.axis_size("core"))
    return lax.ppermute(block, (axis, "core"), route(sizes, lambda i, c: (i + way * (1 - 2 * c), c)))


def ring_gather(block, axis):
    size = lax.axis_size(axis)
    ahead, behind = [block], [block]
    for _ in range(size // 2):
        ahead.append(ring(ahead[-1], axis))
    for _ in range((size - 1) // 2):
        behind.append(ring(behind[-1], axis, -1))
    return ahead + behind[:0:-1]


def add(*terms):
    return sum(t.astype(jnp.float32) for t in terms).astype(jnp.bfloat16)


def ring_reduce(piece, place, up, axis):
    size = lax.axis_size(axis)
    sums = []
    for way, steps in ((1, size // 2), (-1, (size - 1) // 2)):
        total = piece(place + way * up * steps)
        for s in range(1, steps + 1):
            total = ring(total, axis, way)
            if s < steps:
                total = add(total, piece(place + way * up * (steps - s)))
        sums.append(total)
    return add(piece(place), *sums)


def shift(block, q):
    sizes = lax.axis_size("y_lo") * lax.axis_size("z")

    def by(distance):
        pairs = [(i, (i + distance) % sizes) for i in range(sizes)]
        return lambda b: lax.ppermute(b, ("y_lo", "z"), pairs) if distance else b

    return lax.switch(jnp.mod(q, sizes), [by(d) for d in range(sizes)], block)


def turn_kernel(table, near, far, near_out, far_out):
    for amps, out in ((near, near_out), (far, far_out)):
        roots, points, share, columns = amps.shape
        for root in range(roots):
            rows = amps[root].astype(jnp.float32).reshape(points * share, columns)
            out[root * columns : (root + 1) * columns] = rows.T.astype(out.dtype)


def dot2_kernel(pieces, table, mine, other, *refs):
    parts, (amps, row_gap, col) = refs[:pieces], refs[pieces : pieces + 3]
    out, cycle = refs[-2:]
    _, points, _, columns = amps.shape
    share = row_gap.shape[2]
    each = columns // parts[0].shape[0]
    step = pl.program_id(0)

    @pl.when(step == 0)
    def _():
        for s in range(pieces):
            cycle[table[s]] = parts[s][...]

    weights = cycle[pl.ds(step * each, each)].reshape(columns, cycle.shape[2])
    for h, half in enumerate((mine, other)):
        total = lax.dot_general(half[...], weights, (((1,), (1,)), ((), ())), preferred_element_type=jnp.float32)
        count = total.shape[0] // (points * share)
        for p in range(count):
            place = table[pieces + h * count + p]
            rows = pl.ds(pl.multiple_of(place * share, share), share)
            gap = row_gap[place] + col[...][None]
            cyc = total[p * points * share : (p + 1) * points * share].reshape(points, share, columns)
            out[0, :, rows, :] = (cyc + gap * amps[0, :, rows, :].astype(jnp.float32)).astype(out.dtype)


def local(factors, amps, eps_occ, eps_vir, col_energy, q_index):
    y_hi, x, core, z = (lax.axis_index(a) for a in ("y_hi", "x", "core", "z"))
    x_count, z_count, y_count = lax.axis_size("x"), lax.axis_size("z"), lax.axis_size("y_hi")
    amp_local = amps[:, 0]
    roots, points, virtuals, columns = amp_local.shape
    aux = factors.shape[3]
    up = 1 - 2 * core

    share = factors.shape[2]
    places_count = virtuals // share
    held = points * share
    row = jnp.broadcast_to(jnp.pad(eps_vir, ((0, 0), (0, aux - virtuals))), (share, aux))
    shifted = shift(jnp.concatenate([factors[0].reshape(held, aux), row]), q_index[0])
    places = []
    for sign, own_core in ((up, core), (-up, 1 - core)):
        for h in range(y_count):
            for s in range(x_count):
                chip = jnp.mod(y_hi + h, y_count) * x_count + jnp.mod(x - sign * s, x_count)
                places.append(chip * 2 + own_core)
    order = [jnp.mod(z - up * s, z_count) for s in range(z_count)]
    table = jnp.stack(order + places).astype(jnp.int32)

    half = places_count // 2
    turn_spec = lambda first: pl.BlockSpec((roots, points, share, columns), lambda p, t: (0, 0, t[z_count + first + p], 0))
    turn = pl.pallas_call(
        turn_kernel,
        out_shape=[jax.ShapeDtypeStruct((roots * columns, half * held), jnp.bfloat16)] * 2,
        grid_spec=pltpu.PrefetchScalarGridSpec(
            num_scalar_prefetch=1,
            grid=(half,),
            in_specs=[turn_spec(0), turn_spec(half)],
            out_specs=[pl.BlockSpec((roots * columns, held), lambda p, t: (0, p))] * 2,
        ),
        compiler_params=pltpu.CompilerParams(vmem_limit_bytes=16 << 20),
        cost_estimate=pl.CostEstimate(flops=0, bytes_accessed=4 * roots * columns * points * virtuals, transcendentals=0),
        name="turn",
    )

    amp_local = pltpu.with_memory_space_constraint(amp_local, pltpu.HBM)
    own, vir = lax.optimization_barrier((shifted[:held], shifted[held, :virtuals]))
    row_gap = vir.astype(jnp.float32).reshape(places_count, 1, share, 1) - eps_occ[0].reshape(1, points, 1, 1)
    far = swap(own, "y_hi")
    own_ahead = ring(own, "x")
    own_behind = ring(own, "x", -1)
    amp_turned, _ = lax.optimization_barrier((amp_local, own))
    near_amps, far_amps = turn(table, amp_turned, amp_turned)
    near_amps, far_amps, own_ahead, far, row_gap = lax.optimization_barrier((near_amps, far_amps, own_ahead, far, row_gap))
    far_ahead = ring(far, "x")
    far_behind = ring(far, "x", -1)
    own_twice = ring(own_ahead, "x")
    far_twice = ring(far_ahead, "x")
    mine = jnp.concatenate([own, own_ahead, own_twice, own_behind, far, far_ahead, far_twice, far_behind])
    other = swap(mine, "core")
    near_terms = jnp.dot(near_amps, mine, preferred_element_type=jnp.float32)

    col = col_energy.reshape(1, columns)
    whole = lambda a: pl.BlockSpec(a.shape, lambda r, t: (0,) * a.ndim)
    in_vmem = pl.BlockSpec(memory_space=pltpu.VMEM)
    group = roots // CHUNKS

    sigma = None
    for c in range(CHUNKS):
        lines = slice(c * group * columns, (c + 1) * group * columns)
        terms = near_terms[lines] + jnp.dot(far_amps[lines], other, preferred_element_type=jnp.float32)
        terms = terms.astype(jnp.bfloat16).reshape(z_count, -1, aux)

        def piece(i):
            return lax.dynamic_index_in_dim(terms, jnp.mod(i, z_count), 0, keepdims=False)

        total = ring_reduce(piece, z, up, "z")
        total = add(total, swap(total, "y_lo"))
        parts = ring_gather(total, "z")

        root_spec = pl.BlockSpec((1, points, virtuals, columns), lambda r, t, first=c * group: (r + first, 0, 0, 0))
        before = [] if sigma is None else [sigma]
        sigma = pl.pallas_call(
            functools.partial(dot2_kernel, z_count),
            out_shape=jax.ShapeDtypeStruct(amp_local.shape, jnp.bfloat16),
            grid_spec=pltpu.PrefetchScalarGridSpec(
                num_scalar_prefetch=1,
                grid=(group,),
                in_specs=[in_vmem] * (2 + z_count)
                + [root_spec, whole(row_gap), whole(col)]
                + [pl.BlockSpec(memory_space=pl.ANY)] * len(before),
                out_specs=root_spec,
                scratch_shapes=[pltpu.VMEM((z_count, *parts[0].shape), jnp.bfloat16)],
            ),
            input_output_aliases={} if sigma is None else {6 + z_count: 0},
            compiler_params=pltpu.CompilerParams(vmem_limit_bytes=16 << 20),
            cost_estimate=pl.CostEstimate(
                flops=2 * points * virtuals * aux * group * columns,
                bytes_accessed=2 * (points * virtuals * (aux + 2 * group * columns) + aux * group * columns),
                transcendentals=0,
            ),
            name="dot2",
        )(table, mine, other, *parts, amp_local, row_gap, col, *before)
    return sigma[:, None]


def solution(mesh):
    split = Mesh(mesh.devices.reshape(2, 8, 2, 4, 2), ("y_lo", "z", "y_hi", "x", "core"))
    kocc, vrow = ("y_lo", "z"), ("y_hi", "x", "core")
    in_specs = (
        P(kocc, None, vrow, None),
        P(None, kocc, None, None, vrow),
        P(kocc, None),
        P(kocc, None),
        P(vrow),
        P(),
    )
    out_specs = P(None, kocc, None, None, vrow)
    return jax.shard_map(local, mesh=split, in_specs=in_specs, out_specs=out_specs, check_vma=False)
```

```python
import functools

import jax
import jax.numpy as jnp
from jax import lax
from jax.experimental import pallas as pl
from jax.experimental.pallas import tpu as pltpu
from jax.sharding import Mesh
from jax.sharding import PartitionSpec as P

CHUNKS = 2


def route(sizes, step):
    pairs = []
    total = 1
    for size in sizes:
        total *= size
    for flat in range(total):
        rest, coords = flat, []
        for size in reversed(sizes):
            coords.insert(0, rest % size)
            rest //= size
        target = 0
        for size, coord in zip(sizes, step(*coords)):
            target = target * size + coord % size
        pairs.append((flat, target))
    return pairs


def swap(block, axis):
    return lax.ppermute(block, axis, [(0, 1), (1, 0)])


def ring(block, axis, way=1):
    sizes = (lax.axis_size(axis), lax.axis_size("core"))
    return lax.ppermute(block, (axis, "core"), route(sizes, lambda i, c: (i + way * (1 - 2 * c), c)))


def ring_gather(block, axis):
    size = lax.axis_size(axis)
    ahead, behind = [block], [block]
    for _ in range(size // 2):
        ahead.append(ring(ahead[-1], axis))
    for _ in range((size - 1) // 2):
        behind.append(ring(behind[-1], axis, -1))
    return ahead + behind[:0:-1]


def add(*terms):
    return sum(t.astype(jnp.float32) for t in terms).astype(jnp.bfloat16)


def ring_reduce(piece, place, up, axis):
    size = lax.axis_size(axis)
    sums = []
    for way, steps in ((1, size // 2), (-1, (size - 1) // 2)):
        total = piece(place + way * up * steps)
        for s in range(1, steps + 1):
            total = ring(total, axis, way)
            if s < steps:
                total = add(total, piece(place + way * up * (steps - s)))
        sums.append(total)
    return add(piece(place), *sums)


def shift(block, q):
    sizes = lax.axis_size("y_lo") * lax.axis_size("z")

    def by(distance):
        pairs = [(i, (i + distance) % sizes) for i in range(sizes)]
        return lambda b: lax.ppermute(b, ("y_lo", "z"), pairs) if distance else b

    return lax.switch(jnp.mod(q, sizes), [by(d) for d in range(sizes)], block)


def turn_kernel(table, near, far, near_out, *far_outs):
    each = far.shape[0] // len(far_outs)
    for root in range(near.shape[0]):
        lines = lambda first: pl.ds(first * near.shape[-1], near.shape[-1])
        for amps, out, place in ((near, near_out, root), (far, far_outs[root // each], root % each)):
            _, points, share, columns = amps.shape
            rows = amps[root].astype(jnp.float32).reshape(points * share, columns)
            out[lines(place)] = rows.T.astype(out.dtype)


def dot2_kernel(pieces, table, mine, other, *refs):
    parts, (amps, row_gap, col) = refs[:pieces], refs[pieces : pieces + 3]
    out, cycle = refs[-2:]
    _, points, _, columns = amps.shape
    share = row_gap.shape[2]
    each = columns // parts[0].shape[0]
    step = pl.program_id(0)

    @pl.when(step == 0)
    def _():
        for s in range(pieces):
            cycle[table[s]] = parts[s][...]

    weights = cycle[pl.ds(step * each, each)].reshape(columns, cycle.shape[2])
    for h, half in enumerate((mine, other)):
        total = lax.dot_general(half[...], weights, (((1,), (1,)), ((), ())), preferred_element_type=jnp.float32)
        count = total.shape[0] // (points * share)
        for p in range(count):
            place = table[pieces + h * count + p]
            rows = pl.ds(pl.multiple_of(place * share, share), share)
            gap = row_gap[place] + col[...][None]
            cyc = total[p * points * share : (p + 1) * points * share].reshape(points, share, columns)
            out[0, :, rows, :] = (cyc + gap * amps[0, :, rows, :].astype(jnp.float32)).astype(out.dtype)


def local(factors, amps, eps_occ, eps_vir, col_energy, q_index):
    y_hi, x, core, z = (lax.axis_index(a) for a in ("y_hi", "x", "core", "z"))
    x_count, z_count, y_count = lax.axis_size("x"), lax.axis_size("z"), lax.axis_size("y_hi")
    amp_local = amps[:, 0]
    roots, points, virtuals, columns = amp_local.shape
    aux = factors.shape[3]
    up = 1 - 2 * core

    share = factors.shape[2]
    places_count = virtuals // share
    held = points * share
    row = jnp.tile(eps_vir, (share, aux // virtuals))
    shifted = shift(jnp.concatenate([factors[0].reshape(held, aux), row]), q_index[0])
    places = []
    for sign, own_core in ((up, core), (-up, 1 - core)):
        for h in range(y_count):
            for s in range(x_count):
                chip = jnp.mod(y_hi + h, y_count) * x_count + jnp.mod(x - sign * s, x_count)
                places.append(chip * 2 + own_core)
    order = [jnp.mod(z - up * s, z_count) for s in range(z_count)]
    table = jnp.stack(order + places).astype(jnp.int32)

    half = places_count // 2
    group = roots // CHUNKS
    turned_roots = [roots] + [group] * CHUNKS
    turn_spec = lambda first: pl.BlockSpec((roots, points, share, columns), lambda p, t: (0, 0, t[z_count + first + p], 0))
    turn = pl.pallas_call(
        turn_kernel,
        out_shape=[jax.ShapeDtypeStruct((n * columns, half * held), jnp.bfloat16) for n in turned_roots],
        grid_spec=pltpu.PrefetchScalarGridSpec(
            num_scalar_prefetch=1,
            grid=(half,),
            in_specs=[turn_spec(0), turn_spec(half)],
            out_specs=[pl.BlockSpec((n * columns, held), lambda p, t: (0, p)) for n in turned_roots],
        ),
        compiler_params=pltpu.CompilerParams(vmem_limit_bytes=16 << 20),
        cost_estimate=pl.CostEstimate(flops=0, bytes_accessed=4 * roots * columns * points * virtuals, transcendentals=0),
        name="turn",
    )

    amp_local = pltpu.with_memory_space_constraint(amp_local, pltpu.HBM)
    own, vir = lax.optimization_barrier((shifted[:held], shifted[held, :virtuals]))
    row_gap = vir.astype(jnp.float32).reshape(places_count, 1, share, 1) - eps_occ[0].reshape(1, points, 1, 1)
    far = swap(own, "y_hi")
    own_ahead = ring(own, "x")
    own_behind = ring(own, "x", -1)
    amp_turned, _ = lax.optimization_barrier((amp_local, own))
    near_amps, *far_amps = turn(table, amp_turned, amp_turned)
    near_amps, far_amps, own_ahead, far, row_gap = lax.optimization_barrier((near_amps, far_amps, own_ahead, far, row_gap))
    far_ahead = ring(far, "x")
    far_behind = ring(far, "x", -1)
    own_twice = ring(own_ahead, "x")
    far_twice = ring(far_ahead, "x")
    mine = jnp.concatenate([own, own_ahead, own_twice, own_behind, far, far_ahead, far_twice, far_behind])
    other = swap(mine, "core")
    near_terms = jnp.dot(near_amps, mine, preferred_element_type=jnp.float32)

    col = col_energy.reshape(1, columns)
    whole = lambda a: pl.BlockSpec(a.shape, lambda r, t: (0,) * a.ndim)
    in_vmem = pl.BlockSpec(memory_space=pltpu.VMEM)

    sigma = None
    for c in range(CHUNKS):
        lines = slice(c * group * columns, (c + 1) * group * columns)
        terms = near_terms[lines] + jnp.dot(far_amps[c], other, preferred_element_type=jnp.float32)
        terms = terms.astype(jnp.bfloat16).reshape(z_count, -1, aux)

        def piece(i):
            return lax.dynamic_index_in_dim(terms, jnp.mod(i, z_count), 0, keepdims=False)

        total = ring_reduce(piece, z, up, "z")
        total = add(total, swap(total, "y_lo"))
        parts = ring_gather(total, "z")

        root_spec = pl.BlockSpec((1, points, virtuals, columns), lambda r, t, first=c * group: (r + first, 0, 0, 0))
        before = [] if sigma is None else [sigma]
        sigma = pl.pallas_call(
            functools.partial(dot2_kernel, z_count),
            out_shape=jax.ShapeDtypeStruct(amp_local.shape, jnp.bfloat16),
            grid_spec=pltpu.PrefetchScalarGridSpec(
                num_scalar_prefetch=1,
                grid=(group,),
                in_specs=[in_vmem] * (2 + z_count)
                + [root_spec, whole(row_gap), whole(col)]
                + [pl.BlockSpec(memory_space=pl.ANY)] * len(before),
                out_specs=root_spec,
                scratch_shapes=[pltpu.VMEM((z_count, *parts[0].shape), jnp.bfloat16)],
            ),
            input_output_aliases={} if sigma is None else {6 + z_count: 0},
            compiler_params=pltpu.CompilerParams(vmem_limit_bytes=16 << 20),
            cost_estimate=pl.CostEstimate(
                flops=2 * points * virtuals * aux * group * columns,
                bytes_accessed=2 * (points * virtuals * (aux + 2 * group * columns) + aux * group * columns),
                transcendentals=0,
            ),
            name="dot2",
        )(table, mine, other, *parts, amp_local, row_gap, col, *before)
    return sigma[:, None]


def solution(mesh):
    split = Mesh(mesh.devices.reshape(2, 8, 2, 4, 2), ("y_lo", "z", "y_hi", "x", "core"))
    kocc, vrow = ("y_lo", "z"), ("y_hi", "x", "core")
    in_specs = (
        P(kocc, None, vrow, None),
        P(None, kocc, None, None, vrow),
        P(kocc, None),
        P(kocc, None),
        P(vrow),
        P(),
    )
    out_specs = P(None, kocc, None, None, vrow)
    return jax.shard_map(local, mesh=split, in_specs=in_specs, out_specs=out_specs, check_vma=False)
```
